32 devices in a mesh: row: 4 (over y, x), col: 8 (over z, core).
Axes of the slice: x: 2, y: 2, z: 4, core: 2. Of those that a mesh axis runs over, the one named last changes fastest.
Arguments:
- integrals: bfloat16 [800, 800, 640], P('row', 'col'), may hold values from -0.625 to 0.625
- amplitudes: bfloat16 [1024, 640], P('row', 'col'), may hold values from -6 to 6
- virt_irrep: int32 [800], replicated, may hold values from 0 to 7, as said below
- pair_irrep: int32 [640], replicated, may hold values from 0 to 7, as said below
- virt_energy: float32 [800], replicated, may hold values from 0.3 to 4
- occ_energy: float32 [32], replicated, may hold values from -2 to -0.3
Outputs:
- update: bfloat16 [800, 800, 1024], P('row', 'col')
The draws below stay inside these ranges and needn't reach their ends.
Inputs may be any that keep to these rules, and one draw needn't show every extreme that they name: `virt_irrep`: labels never fall along the index; each of the 8 labels covers one contiguous run of at least 66 orbitals. `pair_irrep`: labels never fall along the index; each of the 8 labels covers one contiguous run of at least 53 pairs.
All inputs are finite; a program needn't handle non-finite values.
Results may differ from the reference program's by a relative error of at most 0.0049.
Values may be sent and summed in bfloat16 or wider, within the bound.
No kernel may reach another device: no remote copies, remote signals or barrier semaphores. Data moves between devices by JAX's collectives and lax.ppermute only.
A program may use at most 320 MiB of HBM per device.

```python
import math
import jax
import jax.numpy as jnp
from jax import lax

VIRT = 800
OCC = 32
CD = 640
PAIRS = 1024


def blocked_labels(key, total):
    least = total // 12
    spare = total - 8 * least
    labels = jnp.arange(8, dtype=jnp.int32)
    picks = jax.random.randint(key, (spare,), 0, 8)
    counts = least + jnp.sum((picks[:, None] == labels[None, :]).astype(jnp.int32), axis=0)
    ends = jnp.cumsum(counts).astype(jnp.int32)
    position = jnp.arange(total, dtype=jnp.int32)
    return jnp.sum((position[:, None] >= ends[None, :7]).astype(jnp.int32), axis=1).astype(jnp.int32)


def draw_virt_irrep(key, part):
    return blocked_labels(jax.random.fold_in(key, 11), VIRT)


def draw_pair_irrep(key, part):
    return blocked_labels(jax.random.fold_in(key, 23), CD)


def level_of(key, dims, cuts, smallest, high):
    gain = 1.0
    for axis_at, parts in cuts:
        steps = jax.random.uniform(jax.random.fold_in(jax.random.fold_in(key, 6), axis_at), (parts,), jnp.float32, smallest / len(cuts), high / len(cuts))
        gain = gain * jnp.repeat(jnp.exp(steps), dims[axis_at] // parts).reshape((-1,) + (1,) * (len(dims) - 1 - axis_at))
    return gain


def normal_values(key, extent, spread, reach, pieces=(), kind=jnp.bfloat16):
    drawn = jax.random.normal(key, extent, jnp.float32) * spread
    if len(pieces) > 0:
        drawn = level_of(key, extent, pieces, -0.22, 0.18) * drawn
    return jnp.clip(drawn, min=-reach, max=reach).astype(kind)


def setup_inputs(seed: int = 0) -> dict:
    splits = jax.random.split(jax.random.key(seed), 7)
    integrals = normal_values(splits[0], (VIRT, VIRT, CD), (CD // 8) ** -0.5, 0.625, ((0, 4), (1, 8)))
    amplitudes = normal_values(splits[1], (PAIRS, CD), 1.0, 6.0, ((0, 4), (1, 8)))
    virt_irrep = draw_virt_irrep(jax.random.fold_in(splits[6], 71), 0)
    pair_irrep = draw_pair_irrep(jax.random.fold_in(splits[6], 71), 0)
    virt_energy = jnp.clip(jnp.exp(jax.random.uniform(splits[4], (VIRT,), jnp.float32, math.log(0.3), math.log(4.0))), 0.3, 4.0)
    occ_energy = jnp.clip(jax.random.uniform(splits[5], (OCC,), jnp.float32, -2.0, -0.3), -2.0, -0.3)
    return dict(integrals=integrals, amplitudes=amplitudes, virt_irrep=virt_irrep, pair_irrep=pair_irrep, virt_energy=virt_energy, occ_energy=occ_energy)


def reference(integrals, amplitudes, virt_irrep, pair_irrep, virt_energy, occ_energy):
    width = VIRT // 16
    index = jnp.arange(16, dtype=jnp.int32)

    def contract(block):
        rows = lax.dynamic_slice_in_dim(integrals, block * width, width, 0)
        labels = lax.dynamic_slice_in_dim(virt_irrep, block * width, width, 0)
        keep = jnp.bitwise_xor(labels[:, None, None], virt_irrep[None, :, None]) == pair_irrep[None, None, :]
        masked = jnp.where(keep, rows, jnp.zeros((), rows.dtype))
        total = lax.dot_general(masked.reshape(width * VIRT, CD), amplitudes, (((1,), (1,)), ((), ())), preferred_element_type=jnp.float32)
        return total.astype(jnp.bfloat16).reshape(width, VIRT, PAIRS)

    ladder = lax.map(contract, index).reshape(VIRT, VIRT, PAIRS)
    pair_energy = (occ_energy[:, None] + occ_energy[None, :]).reshape(PAIRS)

    def finish(block):
        own = lax.dynamic_slice_in_dim(ladder, block * width, width, 0)
        other = lax.dynamic_slice_in_dim(ladder, block * width, width, 1)
        other = jnp.transpose(other.reshape(VIRT, width, OCC, OCC), (1, 0, 3, 2)).reshape(width, VIRT, PAIRS)
        first = lax.dynamic_slice_in_dim(virt_energy, block * width, width, 0)
        denom = first[:, None, None] + virt_energy[None, :, None] - pair_energy[None, None, :]
        return ((own.astype(jnp.float32) + other.astype(jnp.float32)) / denom).astype(jnp.bfloat16)

    return lax.map(finish, index).reshape(VIRT, VIRT, PAIRS)
```

```python
import functools

import jax
import jax.numpy as jnp
from jax import lax
from jax.experimental import pallas as pl
from jax.experimental.pallas import tpu as pltpu
from jax.sharding import PartitionSpec as P

LABELS = 8
LANES = 128


def round_up(value, step):
    return (value + step - 1) // step * step


def divisor_up_to(total, most):
    return max(n for n in range(1, most + 1) if total % n == 0)


def pack_kernel(lb_ref, shift_ref, la_ref, pair_ref, slot_ref, view_ref, own_ref, turned_ref, lhs, flat):
    count, eight, slab = view_ref.shape
    rows = turned_ref.shape[1]
    width = slot_ref.shape[1]

    @pl.when(pl.program_id(0) == 0)
    def _():
        flat[...] = jnp.zeros_like(flat)
        lhs[...] = jnp.zeros_like(lhs)

    pair = jnp.broadcast_to(pair_ref[...], (eight, slab))

    def one(b):
        run = jnp.bitwise_xor(la_ref[...], lb_ref[b])
        run = jnp.concatenate([run] * (slab // LANES), axis=1)
        return jnp.where(run == pair, view_ref[b].astype(jnp.float32), 0.0)

    def two(n, _):
        both = jnp.concatenate([one(2 * n), one(2 * n + 1)], axis=0)
        at = pl.multiple_of(2 * eight * n, 2 * eight)
        lhs[pl.ds(at, 2 * eight), :] = both.astype(lhs.dtype)
        return _

    lax.fori_loop(0, count // 2, two, None, unroll=5)
    if count % 2:
        last = jnp.concatenate([one(count - 1), jnp.zeros((eight, slab), jnp.float32)], axis=0)
        lhs[(count - 1) * eight : (count + 1) * eight, :] = last.astype(lhs.dtype)
    packed = jnp.dot(lhs[...], slot_ref[...], preferred_element_type=jnp.float32)
    for part in range(width // LANES):
        flat[part, : lhs.shape[0], :] = packed[:, part * LANES : (part + 1) * LANES]
    own_ref[...] = packed[: count * eight].reshape(count, eight, width).astype(own_ref.dtype)
    for j in range(eight):
        for part in range(width // LANES):
            column = pltpu.roll(flat[part, pl.ds(j, rows, stride=eight), :], shift_ref[0], 0)
            turned_ref[j, :, part * LANES : (part + 1) * LANES] = column.astype(turned_ref.dtype)


def pack(view, labels_a, labels_b, pair_irrep, slots, shift, padded_b, padded_a):
    tile_b, tile_a, slab = view.shape
    width = slots.shape[1]
    steps = pl.cdiv(tile_a, 8)
    spread = jnp.broadcast_to(jnp.pad(labels_a, (0, steps * 8 - tile_a))[:, None], (steps * 8, LANES))
    return pl.pallas_call(
        pack_kernel,
        grid_spec=pltpu.PrefetchScalarGridSpec(
            num_scalar_prefetch=2,
            grid=(steps,),
            in_specs=[
                pl.BlockSpec((8, LANES), lambda i, *_: (i, 0)),
                pl.BlockSpec((1, slab), lambda i, *_: (0, 0)),
                pl.BlockSpec((slab, width), lambda i, *_: (0, 0)),
                pl.BlockSpec((tile_b, 8, slab), lambda i, *_: (0, i, 0)),
            ],
            out_specs=[
                pl.BlockSpec((tile_b, 8, width), lambda i, *_: (0, i, 0)),
                pl.BlockSpec((8, padded_b, width), lambda i, *_: (i, 0, 0)),
            ],
            scratch_shapes=[
                pltpu.VMEM((round_up(tile_b, 2) * 8, slab), jnp.bfloat16),
                pltpu.VMEM((width // LANES, max(padded_b, round_up(tile_b, 2)) * 8, LANES), jnp.float32),
            ],
        ),
        out_shape=[
            jax.ShapeDtypeStruct((tile_b, padded_a, width), view.dtype),
            jax.ShapeDtypeStruct((tile_a, padded_b, width), view.dtype),
        ],
        compiler_params=pltpu.CompilerParams(vmem_limit_bytes=48 << 20),
        cost_estimate=pl.CostEstimate(
            flops=2 * tile_a * tile_b * slab * width,
            bytes_accessed=2 * tile_a * tile_b * (slab + 2 * width),
            transcendentals=0,
        ),
        name="pack",
    )(labels_b, shift, spread, pair_irrep[None, :], slots, view)


def ladder_kernel(
    bases, hops, where_ref, la_ref, lb_ref, vb_ref, spread_ref, va_ref, pe_ref, amp_ref, own_ref, *refs
):
    pieces, (out_ref, acc, mir_ref) = refs[:-3], refs[-3:]
    many, tile_a, pairs = out_ref.shape
    width = own_ref.shape[2]
    split = len(bases)
    inner = pl.num_programs(1)
    rows = pieces[0].shape[1]
    take = pl.ds(pl.program_id(1) * many, many)

    def assemble(hop, side):
        for part in range(split):
            piece = pieces[(side ^ part) * hops + hop]
            base = bases[part]
            shared = 0 if part == 0 else bases[part - 1] + rows - base
            if shared > 0:
                both = mir_ref[:, base : base + shared, :].astype(jnp.float32)
                both = both + piece[take, :shared, :].astype(jnp.float32)
                mir_ref[:, base : base + shared, :] = both.astype(mir_ref.dtype)
            mir_ref[:, base + shared : base + rows, :] = piece[take, shared:, :]

    for hop in range(hops):
        for side in range(split):
            pl.when(jnp.logical_and(pl.program_id(0) == hop, where_ref[1] == side))(
                functools.partial(assemble, hop, side)
            )
    first = (jnp.bitwise_xor(pl.program_id(0), where_ref[0]) * inner + pl.program_id(1)) * many
    b_low = lb_ref[first]
    b_high = lb_ref[first + many - 1]

    def tile(at, size):
        own = own_ref[:, pl.ds(at, 16), :].reshape(many * 16, width)
        mir = mir_ref[:, pl.ds(at, 16), :].reshape(many * 16, width)
        lhs = jnp.concatenate([own, mir], axis=1)
        a_low = la_ref[at]
        a_high = la_ref[at + size - 1]
        single = jnp.logical_and(a_low == a_high, b_low == b_high)

        @pl.when(single)
        def _():
            acc[...] = jnp.dot(lhs, amp_ref[jnp.bitwise_xor(a_low, b_low)], preferred_element_type=jnp.float32)

        @pl.when(jnp.logical_not(single))
        def _():
            acc[...] = jnp.zeros_like(acc)
            spread = spread_ref[pl.ds(at, 16), :]

            def over_a(label_a, _):
                def over_b(label_b, _):
                    keep = [
                        jnp.where(lb_ref[first + b] == label_b, spread, -1) == label_a for b in range(many)
                    ]
                    keep = jnp.concatenate(keep, axis=0)
                    keep = jnp.concatenate([keep.astype(jnp.float32)] * (2 * width // LANES), axis=1)
                    part = jnp.where(keep > 0, lhs.astype(jnp.float32), 0.0).astype(lhs.dtype)
                    acc[...] += jnp.dot(
                        part, amp_ref[jnp.bitwise_xor(label_a, label_b)], preferred_element_type=jnp.float32
                    )
                    return _

                return lax.fori_loop(b_low, b_high + 1, over_b, _)

            lax.fori_loop(a_low, a_high + 1, over_a, None)

        energy_a = va_ref[pl.ds(at, 16), :]
        for b in range(many):
            level = energy_a + vb_ref[first + b]
            level = jnp.concatenate([level] * (pairs // LANES), axis=1)
            denom = level - pe_ref[...]
            value = (acc[16 * b : 16 * b + 16, :] / denom).astype(out_ref.dtype)
            out_ref[b, pl.ds(at, size), :] = value[:size]

    whole = tile_a // 16

    def step(n, _):
        tile(pl.multiple_of(16 * n, 16), 16)
        return _

    lax.fori_loop(0, whole, step, None)
    if tile_a % 16:
        tile(whole * 16, tile_a % 16)


def ladder(own, pieces, hops, bases, where, amps, labels_a, labels_b, energy_a, energy_b, pair_energy, tile_a):
    tile_b, padded_a, width = own.shape
    pairs = amps.shape[2]
    run = tile_b // hops
    many = divisor_up_to(run, 25 if width <= LANES else 5)
    inner = run // many
    pad = (0, padded_a - tile_a)
    spread = jnp.broadcast_to(jnp.pad(labels_a, pad)[:, None], (padded_a, LANES))
    spread_energy = jnp.broadcast_to(jnp.pad(energy_a, pad)[:, None], (padded_a, LANES))
    once = pl.Buffered(1)

    def block(i, n, where_ref, *_):
        return (jnp.bitwise_xor(i, where_ref[0]) * inner + n, 0, 0)

    return pl.pallas_call(
        functools.partial(ladder_kernel, bases, hops),
        grid_spec=pltpu.PrefetchScalarGridSpec(
            num_scalar_prefetch=4,
            grid=(hops, inner),
            in_specs=[
                pl.BlockSpec((padded_a, LANES), lambda *_: (0, 0)),
                pl.BlockSpec((padded_a, LANES), lambda *_: (0, 0)),
                pl.BlockSpec((1, pairs), lambda *_: (0, 0)),
                pl.BlockSpec(amps.shape, lambda *_: (0, 0, 0), pipeline_mode=once),
                pl.BlockSpec((many, padded_a, width), block),
            ]
            + [pl.BlockSpec(piece.shape, lambda *_: (0, 0, 0), pipeline_mode=once) for piece in pieces],
            out_specs=pl.BlockSpec((many, tile_a, pairs), block),
            scratch_shapes=[
                pltpu.VMEM((many * 16, pairs), jnp.float32),
                pltpu.VMEM((many, padded_a, width), own.dtype),
            ],
        ),
        out_shape=jax.ShapeDtypeStruct((tile_b, tile_a, pairs), own.dtype),
        compiler_params=pltpu.CompilerParams(vmem_limit_bytes=60 << 20),
        cost_estimate=pl.CostEstimate(
            flops=4 * tile_a * tile_b * width * pairs,
            bytes_accessed=2 * tile_a * tile_b * (2 * width + pairs),
            transcendentals=0,
        ),
        name="ladder",
    )(where, labels_a, labels_b, energy_b, spread, spread_energy, pair_energy[None, :], amps, own, *pieces)


def pair_swapper(occupied):
    pairs = occupied * occupied
    source = jnp.arange(pairs, dtype=jnp.int32)
    target = source % occupied * occupied + source // occupied
    return (source[:, None] == target[None, :]).astype(jnp.bfloat16)


def per_device(rows, cols, integrals, amplitudes, virt_irrep, pair_irrep, virt_energy, occ_energy):
    tile_a, tile_b, slab = integrals.shape
    occupied = occ_energy.shape[0]
    pairs = occupied * occupied
    split = cols // rows
    row_at = lax.axis_index("row")
    col_at = lax.axis_index("col")
    labels_a = lax.dynamic_slice_in_dim(virt_irrep, row_at * tile_a, tile_a, 0)
    labels_b = lax.dynamic_slice_in_dim(virt_irrep, col_at * tile_b, tile_b, 0)
    energy_a = lax.dynamic_slice_in_dim(virt_energy, row_at * tile_a, tile_a, 0)
    energy_b = lax.dynamic_slice_in_dim(virt_energy, col_at * tile_b, tile_b, 0)
    pair_energy = (occ_energy[:, None] + occ_energy[None, :]).reshape(pairs)

    labels = jnp.arange(LABELS, dtype=jnp.int32)
    member = pair_irrep[None, :] == labels[:, None]
    widths = jnp.sum(member.astype(jnp.int32), axis=1)
    starts = jnp.sum((pair_irrep[None, :] < labels[:, None]).astype(jnp.int32), axis=1)
    place = jnp.arange(slab, dtype=jnp.int32) - jnp.sum(jnp.where(member, starts[:, None], 0), axis=0)

    bases = [part * tile_b // 16 * 16 for part in range(split)]
    shifts = [part * tile_b - base for part, base in enumerate(bases)]
    padded_b = round_up(max(shifts) + tile_b, 8)
    padded_a = round_up(max(tile_a, bases[-1] + padded_b), 16)
    shift = jnp.asarray(shifts, jnp.int32)[col_at % split][None]
    view = jnp.transpose(integrals, (1, 0, 2))

    side = col_at % split
    layer = col_at // split
    spreads = cols == rows * split and rows & (rows - 1) == 0 and tile_b % rows == 0

    def move(piece, goal):
        moves = []
        for r in range(rows):
            for c in range(cols):
                to_row, to_layer, to_side = goal(r, c // split, c % split)
                moves.append((r * cols + c, to_row * cols + to_layer * split + to_side))
        return lax.ppermute(piece, ("row", "col"), moves)

    def exchange(turned, hops, apart):
        shape = (split, hops, tile_b // hops) + turned.shape[1:]
        turned = turned.reshape(shape)
        pieces, before = [], None
        for flip in range(split):
            part = lax.dynamic_index_in_dim(turned, jnp.bitwise_xor(side, flip), 0, keepdims=False)
            if hops == 1:
                pieces.append(move(part[0], lambda r, z, k: (z, r, k ^ flip)))
                continue
            chunks = [part[n] for n in range(hops)]
            if before is not None:
                chunks = lax.optimization_barrier((chunks, before))[0]
            first = [chunks[0]] + [
                move(chunks[n], lambda r, z, k, n=n: (r ^ n, z, k)) for n in range(1, hops)
            ]
            before = first[1:]
            ready = [lax.select_n(jnp.bitwise_xor(apart, n), *first) for n in range(hops)]
            second = [ready[0]] + [
                move(ready[n], lambda r, z, k, n=n: (r, z ^ n, k)) for n in range(1, hops)
            ]
            ready = [lax.select_n(jnp.bitwise_xor(apart, n), *second) for n in range(hops)]
            for n in range(hops):
                if n == 0 and flip == 0:
                    pieces.append(ready[n])
                else:
                    pieces.append(move(ready[n], lambda r, z, k, n=n: (r ^ n, z, k ^ flip)))
        return pieces

    def run(width, hops):
        apart = jnp.bitwise_xor(row_at, layer) if hops > 1 else jnp.int32(0)
        slots = (place[:, None] == jnp.arange(width, dtype=jnp.int32)[None, :]).astype(integrals.dtype)
        own, turned = pack(view, labels_a, labels_b, pair_irrep, slots, shift, padded_b, padded_a)
        pieces = exchange(turned, hops, apart)
        depth, share = amplitudes.shape[1], amplitudes.shape[0]
        gathered = lax.all_gather(amplitudes.T, ("row", "col"), axis=0)
        gathered = gathered.reshape(rows, cols, depth, share).transpose(1, 2, 0, 3).reshape(slab, pairs)
        swapped = jnp.dot(gathered, pair_swapper(occupied), preferred_element_type=jnp.float32).astype(
            gathered.dtype
        )
        both = jnp.pad(jnp.stack([gathered, swapped]), ((0, 0), (0, width), (0, 0)))
        amps = jnp.stack(
            [lax.dynamic_slice(both, (0, starts[g], 0), (2, width, pairs)) for g in range(LABELS)]
        ).reshape(LABELS, 2 * width, pairs)
        where = jnp.stack([apart, side])
        return ladder(own, pieces, hops, bases, where, amps, labels_a, labels_b, energy_a, energy_b, pair_energy, tile_a)

    widest = jnp.max(widths)
    out = lax.cond(
        widest <= LANES, lambda: run(LANES, rows if spreads else 1), lambda: run(3 * LANES, 1)
    )
    return jnp.transpose(out, (1, 0, 2))


def solution(mesh):
    rows, cols = mesh.shape["row"], mesh.shape["col"]
    return jax.shard_map(
        functools.partial(per_device, rows, cols),
        mesh=mesh,
        in_specs=(P("row", "col", None), P("row", "col"), P(), P(), P(), P()),
        out_specs=P("row", "col", None),
        check_vma=False,
    )
```
